128 devices in a mesh: row: 8 (over z, core), col: 16 (over y, x).
Axes of the slice: x: 4, y: 4, z: 4, core: 2. Of those that a mesh axis runs over, the one named last changes fastest.
Arguments:
- snapshots: bfloat16 [4096, 32768], P('row', 'col'), may hold values from -14 to 14
- neighbours: int32 [4096, 128], P('row'), may hold values from 0 to 4095, all different within a row
- start_basis: float32 [32, 4096], replicated, may hold values from -6 to 6
Outputs:
- basis: float32 [32, 4096], P(None, 'row')
- rayleigh: float32 [32, 32], replicated
The draws below stay inside these ranges and needn't reach their ends.
Inputs may be any that keep to these rules, and one draw needn't show every extreme that they name: `neighbours`: each row names 128 different snapshots.
All inputs are finite; a program needn't handle non-finite values.
Results may differ from the reference program's by a relative error of at most 0.00145.
Values may be sent and summed in bfloat16 or wider, within the bound.
No kernel may reach another device: no remote copies, remote signals or barrier semaphores. Data moves between devices by JAX's collectives and lax.ppermute only.
A program may use at most 128 MiB of HBM per device.

```python
import math
import jax
import jax.numpy as jnp
from jax import lax

FEATURES = 32768
LAGS = 64
KNN = 128
RANK = 32
ITERS = 2
SNAPS = 4096


def draw_snapshots(key, part):
    first, second, third, fourth, fifth = jax.random.split(key, 5)
    phase = jax.random.uniform(first, (), jnp.float32, 0.0, 2.0 * math.pi)
    times = jnp.arange(SNAPS, dtype=jnp.float32)
    jitter = jax.random.uniform(second, (SNAPS,), jnp.float32, -1.0, 1.0)
    amplitude = jnp.exp(0.5 * jnp.sin(2.0 * math.pi * times / (3.0 * LAGS) + phase) + 0.3 * jitter)
    log_period = jax.random.uniform(fourth, (FEATURES,), jnp.float32, math.log(4.0), math.log(4.0 * SNAPS))
    cycles = jnp.exp(-log_period)
    offsets = jax.random.uniform(fifth, (FEATURES,), jnp.float32, 0.0, 2.0 * math.pi)
    turns = times[:, None] * cycles[None, :]
    fraction = turns - jnp.floor(turns)
    wave = math.sqrt(2.0) * jnp.cos(2.0 * math.pi * fraction + offsets[None, :])
    noise = jnp.clip(jax.random.normal(third, (SNAPS, FEATURES), jnp.float32), -6.0, 6.0)
    values = wave + 0.3 * noise
    return (amplitude[:, None] * values).astype(jnp.bfloat16)


def choose_distinct(rng, rows, count, top, lift):
    order = jax.random.permutation(jax.random.fold_in(rng, 1), count)
    favour = order
    for power in range(3):
        favour = favour * favour // count
    favour = favour * lift // count
    chance = jax.random.randint(jax.random.fold_in(rng, 2), (rows, count), 0, 4096) + favour
    sure = jax.random.permutation(jax.random.fold_in(rng, 3), rows)[jnp.arange(count) % rows]
    chance = jnp.where(jnp.arange(rows)[:, None] == sure[None, :], 1 << 14, chance)
    score = chance * count + jnp.arange(count)
    return lax.top_k(score.astype(jnp.int32), top)[1].astype(jnp.int32)


def normal_values(stream_key, shape, scale, most, kind=jnp.bfloat16):
    values = scale * jax.random.normal(stream_key, shape, jnp.float32)
    return jnp.clip(values, min=-most, max=most).astype(kind)


def setup_inputs(seed: int = 0) -> dict:
    arg_keys = jax.random.split(jax.random.key(seed), 4)
    return {
        "snapshots": draw_snapshots(jax.random.fold_in(arg_keys[3], 71), 0),
        "neighbours": choose_distinct(arg_keys[1], SNAPS, SNAPS, KNN, 256),
        "start_basis": normal_values(arg_keys[2], (RANK, SNAPS), 1.0, 6.0, jnp.float32),
    }


def apply_operator(basis_rows, markov, neighbours):
    gathered = jnp.take(basis_rows, neighbours, axis=1)
    return jnp.einsum('ris,is->ri', gathered, markov, precision=lax.Precision.HIGHEST)

def reference(snapshots, neighbours, start_basis):
    norms = jnp.sum(jnp.square(snapshots.astype(jnp.float32)), axis=1)
    inner = jnp.dot(snapshots.astype(jnp.float32), snapshots.T.astype(jnp.float32), preferred_element_type=jnp.float32)
    single = norms[:, None] + norms[None, :] - 2.0 * inner
    padded = jnp.pad(single, ((LAGS, 0), (LAGS, 0)))
    window = 1
    while window < LAGS:
        padded = padded[window:, window:] + padded[:-window, :-window]
        window = window * 2
    lagged = padded[1:, 1:]
    chosen = jnp.take_along_axis(lagged.T, neighbours, axis=1)
    slot_kernel = 1.0 / (1.0 + chosen / (LAGS * FEATURES))
    mass = jnp.sum(slot_kernel, axis=1)
    markov = slot_kernel / mass[:, None]
    basis = start_basis
    for step in range(ITERS):
        image = apply_operator(basis, markov, neighbours)
        gram_small = jnp.dot(image.astype(jnp.float32), image.T.astype(jnp.float32), precision=lax.Precision.HIGHEST, preferred_element_type=jnp.float32) / SNAPS
        lower = jnp.linalg.cholesky(gram_small)
        basis = jax.scipy.linalg.solve_triangular(lower, image, lower=True)
    image = apply_operator(basis, markov, neighbours)
    rayleigh = jnp.dot(basis.astype(jnp.float32), image.T.astype(jnp.float32), precision=lax.Precision.HIGHEST, preferred_element_type=jnp.float32) / SNAPS
    return (basis, rayleigh)
```

```python
import functools

import jax
import jax.numpy as jnp
from jax import lax
from jax.experimental import pallas as pl
from jax.experimental.pallas import tpu as pltpu
from jax.sharding import PartitionSpec as P

SNAPS = 4096
FEATURES = 32768
LAGS = 64
BLOCK = 512
MB = 32
PAD = SNAPS + 128
NT = (((1,), (1,)), ((), ()))
F32 = jnp.float32
BF16 = jnp.bfloat16


def row_perm(step, flip):
    return [(2 * z + c, 2 * ((z + step) % 4) + (c ^ flip)) for z in range(4) for c in range(2)]


def col_perm(dy, dx):
    return [(4 * y + x, 4 * ((y + dy) % 4) + (x + dx) % 4) for y in range(4) for x in range(4)]


def half_squares(x):
    f = x.astype(F32)
    q = 0.5 * f * f
    hi = q.astype(BF16)
    return hi, (q - hi.astype(F32)).astype(BF16)


def pick_kernel(where_ref, p0, p1, p2, p3, q0, q1, q2, q3, nb_ref, out_ref, x_ref, nj_ref, nt_ref, g_ref, ring_ref, s_ref, sem):
    step = pl.program_id(0)
    z = where_ref[0]
    par = where_ref[1]
    lane = lax.broadcasted_iota(jnp.int32, (8, 128), 1)

    def block_rows(d, parity):
        b = 2 * lax.rem(z + d, 4) + parity
        return pl.ds(pl.multiple_of(b * BLOCK, BLOCK), BLOCK)

    @pl.when(step == 0)
    def _():
        copies = []
        for d, (p, q) in enumerate(((p0, q0), (p1, q1), (p2, q2), (p3, q3))):
            copies.append(pltpu.make_async_copy(p, x_ref.at[block_rows(d, par)], sem.at[d]))
            copies.append(pltpu.make_async_copy(q, x_ref.at[block_rows(d, 1 - par)], sem.at[4 + d]))
        for c in copies:
            c.start()
        s_ref[...] = jnp.zeros_like(s_ref)
        for c in copies:
            c.wait()
        ones = jnp.ones((8, BLOCK), BF16)
        for b in range(16):
            hi, lo = half_squares(x_ref[b * 256 : (b + 1) * 256, :])
            nj_ref[:, b * 256 : (b + 1) * 256] = lax.dot_general(
                ones, hi, NT, preferred_element_type=F32
            ) + lax.dot_general(ones, lo, NT, preferred_element_type=F32)

    m0 = (step - 2) * MB
    rows = []
    for a in range(8):
        t = 1024 * lax.rem(z + a // 2, 4) + BLOCK * par + 256 * (a % 2) + m0
        t = jnp.maximum(t, 0)
        rows.append(x_ref[pl.ds(pl.multiple_of(t, MB), MB), :])
    lhs = jnp.concatenate(rows, 0)
    ri = lax.broadcasted_iota(jnp.int32, (256, 256), 0)
    ci = lax.broadcasted_iota(jnp.int32, (256, 256), 1)
    perm = jnp.where(ci == lax.rem(ri, 8) * MB + lax.div(ri, 8), 1.0, 0.0).astype(BF16)
    lhs = jnp.dot(perm, lhs, preferred_element_type=F32).astype(BF16)
    ones = jnp.ones((BLOCK, 128), BF16)
    hi, lo = half_squares(lhs)
    nt_ref[...] = jnp.dot(hi, ones, preferred_element_type=F32) + jnp.dot(lo, ones, preferred_element_type=F32)
    for jb in range(8):
        r = lax.dot_general(lhs, x_ref[jb * BLOCK : (jb + 1) * BLOCK, :], NT, preferred_element_type=F32)
        for k in range(4):
            g_ref[jb * 4 + k] = r[:, k * 128 : (k + 1) * 128]

    def run(base, halo):
        def body(mi, carry):
            m = m0 + mi
            shift = lax.rem(256 - lax.rem(m + 128, 128), 128)
            mask = lane < 128 - lax.rem(m + 128, 128)
            slot = lax.rem(step * MB + mi, LAGS)
            row = pl.ds(pl.multiple_of(mi * 8, 8), 8)
            ring_row = pl.ds(pl.multiple_of(slot * 8, 8), 8)
            nt = nt_ref[row, :]
            if halo:
                sub = lax.broadcasted_iota(jnp.int32, (8, 128), 0)
                first_t = 1024 * lax.rem(z + lax.div(sub, 2), 4) + BLOCK * par + 256 * lax.rem(sub, 2)
                valid = first_t + m >= 0
            else:
                p = nb_ref[:, mi, :] - m
                p = jnp.where(p < 0, p + PAD, p)
                hi = lax.shift_right_logical(p, 7)
                lo = p & 127
                acc = jnp.zeros((8, 128), F32)

            def rolled(c):
                if c == 32:
                    return jnp.zeros((8, 128), F32)
                v = (nj_ref[:, c * 128 : (c + 1) * 128] + nt) - g_ref[c, row, :]
                if halo:
                    v = jnp.where(valid, v, 0.0)
                return pltpu.roll(v, shift, 1)

            first = rolled(base % 33)
            cur = first
            for cd in range(33):
                nxt = first if cd == 32 else rolled((cd + base + 1) % 33)
                d = jnp.where(mask, cur, nxt)
                col = slice(cd * 128, (cd + 1) * 128)
                if halo:
                    s = s_ref[:, col] + d
                else:
                    s = s_ref[:, col] + (d - ring_ref[ring_row, col])
                    g = jnp.take_along_axis(s, lo, axis=1, mode="promise_in_bounds")
                    acc = jnp.where(hi == cd, g, acc)
                s_ref[:, col] = s
                ring_ref[ring_row, col] = d
                cur = nxt
            if not halo:
                out_ref[:, mi, :] = acc
            return carry

        lax.fori_loop(0, MB, body, 0)

    pl.when(step < 2)(lambda: run(-1, True))
    pl.when((step >= 2) & (step < 6))(lambda: run(0, False))
    pl.when(step >= 6)(lambda: run(1, False))


def pick(where, own, other, nb):
    anywhere = pl.BlockSpec(memory_space=pl.ANY)
    imap = lambda i, w: (0, jnp.maximum(i - 2, 0), 0)
    return pl.pallas_call(
        pick_kernel,
        grid_spec=pltpu.PrefetchScalarGridSpec(
            num_scalar_prefetch=1,
            grid=(10,),
            in_specs=[anywhere] * 8 + [pl.BlockSpec((8, MB, 128), imap)],
            out_specs=pl.BlockSpec((8, MB, 128), imap),
            scratch_shapes=[
                pltpu.VMEM((SNAPS, BLOCK), BF16),
                pltpu.VMEM((8, SNAPS), F32),
                pltpu.VMEM((256, 128), F32),
                pltpu.VMEM((32, 256, 128), F32),
                pltpu.VMEM((8 * LAGS, PAD), F32),
                pltpu.VMEM((8, PAD), F32),
                pltpu.SemaphoreType.DMA((8,)),
            ],
        ),
        out_shape=jax.ShapeDtypeStruct((8, 256, 128), F32),
        compiler_params=pltpu.CompilerParams(vmem_limit_bytes=40 * 1024 * 1024),
        name="pick",
    )(where, *own, *other, nb)


def slot_map_kernel(nb_ref, out_ref):
    sub32 = lax.broadcasted_iota(jnp.int32, (32, 128), 0)
    sub128 = lax.broadcasted_iota(jnp.int32, (128, 128), 0)
    number = lax.broadcasted_iota(jnp.int32, (32, 128), 1).astype(F32) + 1.0

    def body(t, carry):
        nb = nb_ref[pl.ds(t, 1), :]
        hi = jnp.broadcast_to(lax.shift_right_logical(nb, 7), (32, 128))
        lo = jnp.broadcast_to(nb & 127, (128, 128))
        left = jnp.where(sub32 == hi, number, 0.0).astype(BF16)
        right = jnp.where(sub128 == lo, 1.0, 0.0).astype(BF16)
        out_ref[t] = lax.dot_general(left, right, NT, preferred_element_type=F32).astype(jnp.int32)
        return carry

    lax.fori_loop(0, 64, body, 0, unroll=8)


def slot_map(nb):
    return pl.pallas_call(
        slot_map_kernel,
        grid=(8,),
        in_specs=[pl.BlockSpec((64, 128), lambda i: (i, 0))],
        out_specs=pl.BlockSpec((64, 32, 128), lambda i: (i, 0, 0)),
        out_shape=jax.ShapeDtypeStruct((BLOCK, 32, 128), jnp.int32),
        cost_estimate=pl.CostEstimate(flops=2 * BLOCK * 32 * 128 * 128 * 8, bytes_accessed=9 << 20, transcendentals=0),
        name="slot_map",
    )(nb)


def operator_kernel(sum_ref, map_ref, out_ref):
    kernel = 1.0 / (1.0 + sum_ref[...] * (2.0 / (LAGS * FEATURES)))
    mass = jnp.sum(kernel, axis=1, keepdims=True)
    markov = kernel / mass
    for g in range(8):
        w = markov[g * 8 : (g + 1) * 8, :]
        for c in range(32):
            at = map_ref[g * 8 : (g + 1) * 8, c * 128 : (c + 1) * 128]
            value = jnp.take_along_axis(w, (at - 1) & 127, axis=1, mode="promise_in_bounds")
            out_ref[g * 8 : (g + 1) * 8, c * 128 : (c + 1) * 128] = jnp.where(at > 0, value, 0.0)


def operator(total, slots):
    return pl.pallas_call(
        operator_kernel,
        grid=(8,),
        in_specs=[pl.BlockSpec((64, 128), lambda i: (i, 0)), pl.BlockSpec((64, SNAPS), lambda i: (i, 0))],
        out_specs=pl.BlockSpec((64, SNAPS), lambda i: (i, 0)),
        out_shape=jax.ShapeDtypeStruct((BLOCK, SNAPS), F32),
        name="operator",
    )(total, slots)


def sum_four(v, axis, perms):
    r1, r2, r3 = [lax.ppermute(v, axis, p) for p in perms]
    v, r1, r2, r3 = [a.astype(F32) for a in (v, r1, r2, r3)]
    return (v + r2) + (r1 + r3)


def mul(a, b, dims=(((1,), (0,)), ((), ()))):
    return lax.dot_general(a, b, dims, precision=lax.Precision.HIGHEST, preferred_element_type=F32)


def shards(snapshots, neighbours, start_basis):
    row_at = lax.axis_index("row")
    z = row_at // 2
    par = row_at % 2
    z_send = [row_perm(d, 0) for d in (1, 2, 3)]
    core_swap = row_perm(0, 1)
    width = snapshots.shape[1] // 4

    nb16 = neighbours.astype(jnp.int16)
    nb_from = [neighbours] + [None] * 3
    for d in (1, 2, 3):
        nb_from[4 - d] = lax.ppermute(nb16, "row", z_send[d - 1]).astype(jnp.int32)

    def piece(d):
        at = ((z + d) % 4) * width
        return lax.dynamic_slice_in_dim(snapshots, at, width, 1)

    own = [piece(0)] + [None] * 3
    for d in (1, 3, 2):
        own[4 - d] = lax.ppermute(piece(d), "row", z_send[d - 1])
    other = [lax.ppermute(a, "row", core_swap) for a in own]

    block = neighbours // BLOCK
    relative = (((block % 2) ^ par) * 4 + ((block // 2 - z) % 4)) * BLOCK + neighbours % BLOCK
    slots = slot_map(relative).reshape(BLOCK, SNAPS)
    order = jnp.arange(8, dtype=jnp.int32)
    order = 2 * ((order % 4 + z) % 4) + ((order // 4) ^ par)
    start = jnp.take(start_basis.reshape(32, 8, BLOCK), order, axis=1).reshape(32, SNAPS)

    where = jnp.stack([z, par]).astype(jnp.int32)
    nb_all = jnp.stack(nb_from).reshape(8, 256, 128)
    chosen = pick(where, own, other, nb_all).reshape(4, BLOCK, 128)

    sent = chosen.astype(BF16)
    r1, r2, r3 = [lax.ppermute(sent[d], "row", z_send[d - 1]) for d in (1, 2, 3)]
    total = (chosen[0] + r2.astype(F32)) + (r1.astype(F32) + r3.astype(F32))
    total = sum_four(total.astype(BF16), "col", [col_perm(0, d) for d in (1, 2, 3)])
    total = sum_four(total, "col", [col_perm(d, 0) for d in (1, 2, 3)])

    matrix = operator(total, slots)

    def apply_rows(basis):
        return mul(basis, matrix, NT)

    def gather_all(v):
        parts = [v] + [None] * 3
        for d in (1, 2, 3):
            parts[4 - d] = lax.ppermute(v, "row", z_send[d - 1])
        half = jnp.concatenate(parts, 1)
        gram = (parts[0][:, BLOCK:] + parts[2][:, BLOCK:]) + (parts[1][:, BLOCK:] + parts[3][:, BLOCK:])
        near = jnp.concatenate([p[:, :BLOCK] for p in parts] + [gram], 1)
        far = lax.ppermute(near, "row", core_swap)
        return jnp.concatenate([near[:, :SNAPS // 2], far[:, :SNAPS // 2]], 1), gram + far[:, SNAPS // 2 :]

    image1 = apply_rows(start)
    full1, gram1 = gather_all(jnp.concatenate([image1, mul(image1, image1, NT)], 1))
    image2 = apply_rows(full1)
    full2, gram2 = gather_all(jnp.concatenate([image2, mul(image2, image2, NT)], 1))
    image3 = apply_rows(full2)
    cross = mul(image2, image3, NT)
    cross = sum_four(cross, "row", z_send)
    cross = cross + lax.ppermute(cross, "row", core_swap)

    eye = jnp.eye(32, dtype=F32)
    lower1 = jnp.linalg.cholesky(gram1 / SNAPS)
    inv1 = jax.scipy.linalg.solve_triangular(lower1, eye, lower=True)
    lower2 = jnp.linalg.cholesky(mul(mul(inv1, gram2), inv1, NT) / SNAPS)
    inv = mul(jax.scipy.linalg.solve_triangular(lower2, eye, lower=True), inv1)
    basis = mul(inv, image2)
    rayleigh = mul(mul(inv, cross), inv, NT) / SNAPS
    return basis, rayleigh


def solution(mesh):
    placed = (P("row", "col"), P("row", None), P())
    return jax.shard_map(
        shards, mesh=mesh, in_specs=placed, out_specs=(P(None, "row"), P()), check_vma=False
    )
```

```python
import functools

import jax
import jax.numpy as jnp
from jax import lax
from jax.experimental import pallas as pl
from jax.experimental.pallas import tpu as pltpu
from jax.sharding import PartitionSpec as P

SNAPS = 4096
FEATURES = 32768
LAGS = 64
BLOCK = 512
MB = 32
PAD = SNAPS + 128
GROUP = 8
NT = (((1,), (1,)), ((), ()))
F32 = jnp.float32
BF16 = jnp.bfloat16


def row_perm(step, flip):
    return [(2 * z + c, 2 * ((z + step) % 4) + (c ^ flip)) for z in range(4) for c in range(2)]


def col_perm(dy, dx):
    return [(4 * y + x, 4 * ((y + dy) % 4) + (x + dx) % 4) for y in range(4) for x in range(4)]


def squares(x):
    f = x.astype(F32)
    q = f * f
    hi = q.astype(BF16)
    return hi, (q - hi.astype(F32)).astype(BF16)


def pick_kernel(where_ref, p0, p1, p2, p3, q0, q1, q2, q3, nb_ref, out_ref, x_ref, nj_ref, nt_ref, g_ref, perm_ref, ring_ref, s_ref, carry_ref, acc_ref, sem):
    step = pl.program_id(0)
    z = where_ref[0]
    par = where_ref[1]
    lane = lax.broadcasted_iota(jnp.int32, (8, 128), 1)
    m0 = (step - 2) * MB

    def block_rows(d, parity):
        b = 2 * lax.rem(z + d, 4) + parity
        return pl.ds(pl.multiple_of(b * BLOCK, BLOCK), BLOCK)

    @pl.when(step == 0)
    def _():
        copies = []
        for d, (p, q) in enumerate(((p0, q0), (p1, q1), (p2, q2), (p3, q3))):
            copies.append(pltpu.make_async_copy(p, x_ref.at[block_rows(d, par)], sem.at[d]))
            copies.append(pltpu.make_async_copy(q, x_ref.at[block_rows(d, 1 - par)], sem.at[4 + d]))
        for c in copies:
            c.start()
        carry_ref[...] = jnp.zeros_like(carry_ref)
        ri = lax.broadcasted_iota(jnp.int32, (256, 256), 0)
        ci = lax.broadcasted_iota(jnp.int32, (256, 256), 1)
        perm_ref[...] = jnp.where(ci == lax.rem(ri, 8) * MB + lax.div(ri, 8), 1.0, 0.0).astype(BF16)
        for c in copies:
            c.wait()
        halves = jnp.full((8, BLOCK), 0.5, BF16)
        for b in range(16):
            hi, lo = squares(x_ref[b * 256 : (b + 1) * 256, :])
            nj_ref[:, b * 256 : (b + 1) * 256] = lax.dot_general(
                halves, hi, NT, preferred_element_type=F32
            ) + lax.dot_general(halves, lo, NT, preferred_element_type=F32)

    rows = []
    for a in range(8):
        t = 1024 * lax.rem(z + a // 2, 4) + BLOCK * par + 256 * (a % 2) + m0
        rows.append(x_ref[pl.ds(pl.multiple_of(jnp.maximum(t, 0), MB), MB), :])
    lhs = jnp.dot(perm_ref[...], jnp.concatenate(rows, 0), preferred_element_type=F32).astype(BF16)
    halves = jnp.full((BLOCK, 128), 0.5, BF16)
    hi, lo = squares(lhs)
    nt_ref[...] = jnp.dot(hi, halves, preferred_element_type=F32) + jnp.dot(lo, halves, preferred_element_type=F32)
    for jb in range(8):
        r = lax.dot_general(lhs, x_ref[jb * BLOCK : (jb + 1) * BLOCK, :], NT, preferred_element_type=F32)
        for k in range(4):
            g_ref[jb * 4 + k] = r[:, k * 128 : (k + 1) * 128]

    def window_sums(base, halo, i):
        shifts, masks, nts, valids = [], [], [], []
        ring = ring_ref.at[lax.rem(step, LAGS // MB) * (MB // GROUP) + i]
        sums = s_ref.at[i]
        here = g_ref.at[:, pl.ds(pl.multiple_of(i * (8 * GROUP), 8 * GROUP), 8 * GROUP), :]
        nt_here = nt_ref.at[pl.ds(pl.multiple_of(i * (8 * GROUP), 8 * GROUP), 8 * GROUP), :]
        for u in range(GROUP):
            m = m0 + i * GROUP + u
            shifts.append(lax.rem(256 - lax.rem(m + 128, 128), 128))
            masks.append(lane < 128 - lax.rem(m + 128, 128))
            nts.append(nt_here[u * 8 : u * 8 + 8, :])
            if halo:
                a = lax.broadcasted_iota(jnp.int32, (8, 128), 0)
                first_t = 1024 * lax.rem(z + lax.div(a, 2), 4) + BLOCK * par + 256 * lax.rem(a, 2)
                valids.append(first_t + m >= 0)
        cache = [{} for _ in range(GROUP)]

        def term(u, c):
            v = (nj_ref[:, c * 128 : (c + 1) * 128] + nts[u]) - here[c, u * 8 : u * 8 + 8, :]
            return jnp.where(valids[u], v, 0.0) if halo else v

        def rolled(u, c):
            if c == 32:
                return jnp.zeros((8, 128), F32)
            low = c - c % 2
            if low not in cache[u]:
                both = jnp.concatenate([term(u, low), term(u, low + 1)], 0).astype(BF16)
                both = pltpu.roll(both, shifts[u], 1).astype(F32)
                cache[u][low], cache[u][low + 1] = both[:8], both[8:]
            return cache[u][c]

        for cd in range(33):
            col = slice(cd * 128, (cd + 1) * 128)
            s = carry_ref[:, col]
            for u in range(GROUP):
                row = slice(u * 8, u * 8 + 8)
                d = jnp.where(masks[u], rolled(u, (cd + base) % 33), rolled(u, (cd + base + 1) % 33))
                if halo:
                    s = s + d
                else:
                    s = s + (d - ring[row, col])
                    sums[row, col] = s
                ring[row, col] = d
            carry_ref[:, col] = s

    def look_up(i, u):
        mi = i * GROUP + u
        p = nb_ref[mi] - (m0 + mi)
        p = jnp.where(p < 0, p + PAD, p)
        hi = lax.shift_right_logical(p, 7)
        lo = p & 127
        sums = s_ref.at[i]
        accs = []
        for part in range(3):
            acc = jnp.zeros((8, 128), F32)
            for cd in range(part * 11, part * 11 + 11):
                g = jnp.take_along_axis(sums[u * 8 : u * 8 + 8, cd * 128 : (cd + 1) * 128], lo, axis=1, mode="promise_in_bounds")
                acc = jnp.where(hi == cd, g, acc)
            accs.append(acc)
        acc_ref[pl.ds(pl.multiple_of(mi * 8, 8), 8), :] = jnp.where(hi < 11, accs[0], jnp.where(hi < 22, accs[1], accs[2]))

    def windows(base, halo):
        def body(i, carry):
            window_sums(base, halo, i)
            return carry

        lax.fori_loop(0, MB // GROUP, body, 0)

    pl.when(step < 2)(functools.partial(windows, -1, True))
    pl.when((step >= 2) & (step < 6))(functools.partial(windows, 0, False))
    pl.when(step >= 6)(functools.partial(windows, 1, False))

    @pl.when(step >= 2)
    def _():
        def body(i, carry):
            for u in range(GROUP):
                look_up(i, u)
            return carry

        lax.fori_loop(0, MB // GROUP, body, 0)
        for a in range(8):
            for k in range(MB // 8):
                out_ref[a, k * 8 : (k + 1) * 8, :] = acc_ref[pl.ds(k * 64 + a, 8, stride=8), :]


def pick(where, own, other, nb):
    anywhere = pl.BlockSpec(memory_space=pl.ANY)
    return pl.pallas_call(
        pick_kernel,
        grid_spec=pltpu.PrefetchScalarGridSpec(
            num_scalar_prefetch=1,
            grid=(10,),
            in_specs=[anywhere] * 8
            + [
                pl.BlockSpec((MB, 8, 128), lambda i, w: (jnp.maximum(i - 2, 0), 0, 0)),
            ],
            out_specs=pl.BlockSpec((8, MB, 128), lambda i, w: (0, jnp.maximum(i - 2, 0), 0)),
            scratch_shapes=[
                pltpu.VMEM((SNAPS, BLOCK), BF16),
                pltpu.VMEM((8, SNAPS), F32),
                pltpu.VMEM((256, 128), F32),
                pltpu.VMEM((32, 256, 128), F32),
                pltpu.VMEM((256, 256), BF16),
                pltpu.VMEM((LAGS // GROUP, 8 * GROUP, PAD), F32),
                pltpu.VMEM((MB // GROUP, 8 * GROUP, PAD), F32),
                pltpu.VMEM((8, PAD), F32),
                pltpu.VMEM((256, 128), F32),
                pltpu.SemaphoreType.DMA((8,)),
            ],
        ),
        out_shape=jax.ShapeDtypeStruct((8, 256, 128), F32),
        compiler_params=pltpu.CompilerParams(vmem_limit_bytes=40 * 1024 * 1024),
        name="pick",
    )(where, *own, *other, nb)


def slot_map_kernel(nb_ref, out_ref):
    sub32 = lax.broadcasted_iota(jnp.int32, (32, 128), 0)
    sub128 = lax.broadcasted_iota(jnp.int32, (128, 128), 0)
    number = lax.broadcasted_iota(jnp.int32, (32, 128), 1).astype(F32) + 1.0

    def body(t, carry):
        nb = nb_ref[pl.ds(t, 1), :]
        hi = jnp.broadcast_to(lax.shift_right_logical(nb, 7), (32, 128))
        lo = jnp.broadcast_to(nb & 127, (128, 128))
        left = jnp.where(sub32 == hi, number, 0.0).astype(BF16)
        right = jnp.where(sub128 == lo, 1.0, 0.0).astype(BF16)
        out_ref[t] = lax.dot_general(left, right, NT, preferred_element_type=F32).astype(jnp.int32)
        return carry

    lax.fori_loop(0, 64, body, 0, unroll=8)


def slot_map(nb):
    return pl.pallas_call(
        slot_map_kernel,
        grid=(8,),
        in_specs=[pl.BlockSpec((64, 128), lambda i: (i, 0))],
        out_specs=pl.BlockSpec((64, 32, 128), lambda i: (i, 0, 0)),
        out_shape=jax.ShapeDtypeStruct((BLOCK, 32, 128), jnp.int32),
        cost_estimate=pl.CostEstimate(flops=1 << 20, bytes_accessed=1 << 20, transcendentals=0),
        name="slot_map",
    )(nb)


def split3(x):
    hi = x.astype(BF16)
    rest = x - hi.astype(F32)
    mid = rest.astype(BF16)
    return hi, mid, (rest - mid.astype(F32)).astype(BF16)


def times_transposed(parts, hi, lo):
    r = lax.dot_general(parts, hi, NT, preferred_element_type=F32)
    q = lax.dot_general(parts[:64], lo, NT, preferred_element_type=F32)
    return ((r[64:] + q[32:]) + (r[32:64] + q[:32])) + r[:32]


def operator_kernel(sum_ref, map_ref, b_ref, hi_ref, lo_ref, out_ref):
    kernel = 1.0 / (1.0 + sum_ref[...] * (2.0 / (LAGS * FEATURES)))
    mass = jnp.sum(kernel, axis=1, keepdims=True)
    markov = kernel / mass
    for g in range(8):
        w = [markov[g * 16 + h * 8 : g * 16 + h * 8 + 8, :] for h in range(2)]
        for c in range(32):
            col = slice(c * 128, (c + 1) * 128)
            values = []
            for h in range(2):
                at = map_ref[g * 16 + h * 8 : g * 16 + h * 8 + 8, col]
                value = jnp.take_along_axis(w[h], (at - 1) & 127, axis=1, mode="promise_in_bounds")
                values.append(jnp.where(at > 0, value, 0.0))
            v = jnp.concatenate(values, 0)
            hi = v.astype(BF16)
            hi_ref[g * 16 : (g + 1) * 16, col] = hi
            lo_ref[g * 16 : (g + 1) * 16, col] = (v - hi.astype(F32)).astype(BF16)
    out_ref[...] = times_transposed(jnp.concatenate(split3(b_ref[...]), 0), hi_ref[...], lo_ref[...])


def operator(total, slots, start):
    return pl.pallas_call(
        operator_kernel,
        grid=(4,),
        in_specs=[
            pl.BlockSpec((128, 128), lambda i: (i, 0)),
            pl.BlockSpec((128, SNAPS), lambda i: (i, 0)),
            pl.BlockSpec((32, SNAPS), lambda i: (0, 0)),
        ],
        out_specs=[
            pl.BlockSpec((128, SNAPS), lambda i: (i, 0)),
            pl.BlockSpec((128, SNAPS), lambda i: (i, 0)),
            pl.BlockSpec((32, 128), lambda i: (0, i)),
        ],
        out_shape=[
            jax.ShapeDtypeStruct((BLOCK, SNAPS), BF16),
            jax.ShapeDtypeStruct((BLOCK, SNAPS), BF16),
            jax.ShapeDtypeStruct((32, BLOCK), F32),
        ],
        name="operator",
    )(total, slots, start)


def apply_kernel(hi_ref, lo_ref, *refs):
    pieces, out_ref = refs[:-1], refs[-1]
    halves = len(pieces)
    full = jnp.concatenate([p[:, : SNAPS // halves] for p in pieces], 1)
    out_ref[...] = times_transposed(jnp.concatenate(split3(full), 0), hi_ref[...], lo_ref[...])


def apply_rows(hi, lo, pieces):
    whole = pl.BlockSpec((32, pieces[0].shape[1]), lambda i: (0, 0))
    return pl.pallas_call(
        apply_kernel,
        grid=(2,),
        in_specs=[pl.BlockSpec((256, SNAPS), lambda i: (i, 0))] * 2 + [whole] * len(pieces),
        out_specs=pl.BlockSpec((32, 256), lambda i: (0, i)),
        out_shape=jax.ShapeDtypeStruct((32, BLOCK), F32),
        name="apply",
    )(hi, lo, *pieces)


def sum_four(v, axis, perms):
    r1, r2, r3 = [lax.ppermute(v, axis, p) for p in perms]
    v, r1, r2, r3 = [a.astype(F32) for a in (v, r1, r2, r3)]
    return (v + r2) + (r1 + r3)


def mul(a, b, dims=(((1,), (0,)), ((), ()))):
    return lax.dot_general(a, b, dims, precision=lax.Precision.HIGHEST, preferred_element_type=F32)


def shards(snapshots, neighbours, start_basis):
    row_at = lax.axis_index("row")
    z = row_at // 2
    par = row_at % 2
    z_send = [row_perm(d, 0) for d in (1, 2, 3)]
    core_swap = row_perm(0, 1)
    width = snapshots.shape[1] // 4

    def piece(d):
        at = ((z + d) % 4) * width
        return lax.dynamic_slice_in_dim(snapshots, at, width, 1)

    nb16 = neighbours.astype(jnp.int16)
    nb_from = [neighbours] + [None] * 3
    for d in (1, 2, 3):
        nb_from[4 - d] = lax.ppermute(nb16, "row", z_send[d - 1])
    own = [piece(0)] + [None] * 3
    for d in (2, 1, 3):
        own[4 - d] = lax.ppermute(piece(d), "row", z_send[d - 1])
    other = [lax.ppermute(a, "row", core_swap) for a in own]
    block = neighbours // BLOCK
    relative = (((block % 2) ^ par) * 4 + ((block // 2 - z) % 4)) * BLOCK + neighbours % BLOCK
    slots = slot_map(relative)
    order = jnp.arange(8, dtype=jnp.int32)
    order = 2 * ((order % 4 + z) % 4) + ((order // 4) ^ par)
    start = jnp.take(start_basis.reshape(32, 8, BLOCK), order, axis=1).reshape(32, SNAPS)

    where = jnp.stack([z, par]).astype(jnp.int32)
    nb_all = jnp.stack([a.astype(jnp.int32) for a in nb_from]).reshape(8, 256, 128).transpose(1, 0, 2)
    where, slots = lax.optimization_barrier((where, slots))
    chosen = pick(where, own, other, nb_all).reshape(4, BLOCK, 128)

    sent = chosen.astype(BF16)
    r1, r2, r3 = [lax.ppermute(sent[d], "row", z_send[d - 1]) for d in (1, 2, 3)]
    total = (chosen[0] + r2.astype(F32)) + (r1.astype(F32) + r3.astype(F32))
    total = sum_four(total.astype(BF16), "col", [col_perm(0, d) for d in (1, 2, 3)])
    total = sum_four(total, "col", [col_perm(d, 0) for d in (1, 2, 3)])

    def gather_all(v):
        parts = [v] + [None] * 3
        for d in (1, 2, 3):
            parts[4 - d] = lax.ppermute(v, "row", z_send[d - 1])
        gram = (parts[0][:, BLOCK:] + parts[2][:, BLOCK:]) + (parts[1][:, BLOCK:] + parts[3][:, BLOCK:])
        near = jnp.concatenate([p[:, :BLOCK] for p in parts] + [gram], 1)
        far = lax.ppermute(near, "row", core_swap)
        return (near, far), gram + far[:, SNAPS // 2 :]

    hi, lo, image1 = operator(total, slots.reshape(BLOCK, SNAPS), start)
    full1, gram1 = gather_all(jnp.concatenate([image1, mul(image1, image1, NT)], 1))
    image2 = apply_rows(hi, lo, full1)
    full2, gram2 = gather_all(jnp.concatenate([image2, mul(image2, image2, NT)], 1))
    image3 = apply_rows(hi, lo, full2)
    cross = mul(image2, image3, NT)
    cross = sum_four(cross, "row", z_send)
    cross = cross + lax.ppermute(cross, "row", core_swap)

    eye = jnp.eye(32, dtype=F32)
    lower1 = jnp.linalg.cholesky(gram1 / SNAPS)
    inv1 = jax.scipy.linalg.solve_triangular(lower1, eye, lower=True)
    lower2 = jnp.linalg.cholesky(mul(mul(inv1, gram2), inv1, NT) / SNAPS)
    inv = mul(jax.scipy.linalg.solve_triangular(lower2, eye, lower=True), inv1)
    basis = mul(inv, image2)
    rayleigh = mul(mul(inv, cross), inv, NT) / SNAPS
    return basis, rayleigh


def solution(mesh):
    placed = (P("row", "col"), P("row", None), P())
    return jax.shard_map(
        shards, mesh=mesh, in_specs=placed, out_specs=(P(None, "row"), P()), check_vma=False
    )
```

```python
import functools

import jax
import jax.numpy as jnp
from jax import lax
from jax.experimental import pallas as pl
from jax.experimental.pallas import tpu as pltpu
from jax.sharding import PartitionSpec as P

SNAPS = 4096
FEATURES = 32768
LAGS = 64
BLOCK = 512
MB = 32
PAD = SNAPS + 128
GROUP = 8
NT = (((1,), (1,)), ((), ()))
F32 = jnp.float32
BF16 = jnp.bfloat16


def row_perm(step, flip):
    return [(2 * z + c, 2 * ((z + step) % 4) + (c ^ flip)) for z in range(4) for c in range(2)]


def col_perm(dy, dx):
    return [(4 * y + x, 4 * ((y + dy) % 4) + (x + dx) % 4) for y in range(4) for x in range(4)]


def squares(x):
    f = x.astype(F32)
    q = f * f
    hi = q.astype(BF16)
    return hi, (q - hi.astype(F32)).astype(BF16)


def pick_kernel(where_ref, p0, p1, p2, p3, q0, q1, q2, q3, nb_ref, out_ref, x_ref, nj_ref, nt_ref, g_ref, perm_ref, ring_ref, s_ref, carry_ref, acc_ref, sem):
    step = pl.program_id(0)
    z = where_ref[0]
    par = where_ref[1]
    lane = lax.broadcasted_iota(jnp.int32, (8, 128), 1)
    m0 = (step - 2) * MB

    def block_rows(d, parity):
        b = 2 * lax.rem(z + d, 4) + parity
        return pl.ds(pl.multiple_of(b * BLOCK, BLOCK), BLOCK)

    @pl.when(step == 0)
    def _():
        copies = []
        for d, (p, q) in enumerate(((p0, q0), (p1, q1), (p2, q2), (p3, q3))):
            copies.append(pltpu.make_async_copy(p, x_ref.at[block_rows(d, par)], sem.at[d]))
            copies.append(pltpu.make_async_copy(q, x_ref.at[block_rows(d, 1 - par)], sem.at[4 + d]))
        for c in copies:
            c.start()
        carry_ref[...] = jnp.zeros_like(carry_ref)
        ri = lax.broadcasted_iota(jnp.int32, (256, 256), 0)
        ci = lax.broadcasted_iota(jnp.int32, (256, 256), 1)
        perm_ref[...] = jnp.where(ci == lax.rem(ri, 8) * MB + lax.div(ri, 8), 1.0, 0.0).astype(BF16)
        for c in copies:
            c.wait()
        halves = jnp.full((8, BLOCK), 0.5, BF16)
        for b in range(16):
            hi, lo = squares(x_ref[b * 256 : (b + 1) * 256, :])
            nj_ref[:, b * 256 : (b + 1) * 256] = lax.dot_general(
                halves, hi, NT, preferred_element_type=F32
            ) + lax.dot_general(halves, lo, NT, preferred_element_type=F32)

    rows = []
    for a in range(8):
        t = 1024 * lax.rem(z + a // 2, 4) + BLOCK * par + 256 * (a % 2) + m0
        rows.append(x_ref[pl.ds(pl.multiple_of(jnp.maximum(t, 0), MB), MB), :])
    lhs = jnp.dot(perm_ref[...], jnp.concatenate(rows, 0), preferred_element_type=F32).astype(BF16)
    halves = jnp.full((BLOCK, 128), 0.5, BF16)
    hi, lo = squares(lhs)
    nt_ref[...] = jnp.dot(hi, halves, preferred_element_type=F32) + jnp.dot(lo, halves, preferred_element_type=F32)
    for jb in range(8):
        r = lax.dot_general(lhs, x_ref[jb * BLOCK : (jb + 1) * BLOCK, :], NT, preferred_element_type=F32)
        for k in range(4):
            g_ref[jb * 4 + k] = r[:, k * 128 : (k + 1) * 128]

    def window_sums(base, halo, i):
        shifts, masks, nts, valids = [], [], [], []
        ring = ring_ref.at[lax.rem(step, LAGS // MB) * (MB // GROUP) + i]
        sums = s_ref.at[i]
        here = g_ref.at[:, pl.ds(pl.multiple_of(i * (8 * GROUP), 8 * GROUP), 8 * GROUP), :]
        nt_here = nt_ref.at[pl.ds(pl.multiple_of(i * (8 * GROUP), 8 * GROUP), 8 * GROUP), :]
        for u in range(GROUP):
            m = m0 + i * GROUP + u
            shifts.append(lax.rem(256 - lax.rem(m + 128, 128), 128))
            masks.append(lane < 128 - lax.rem(m + 128, 128))
            nts.append(nt_here[u * 8 : u * 8 + 8, :])
            if halo:
                a = lax.broadcasted_iota(jnp.int32, (8, 128), 0)
                first_t = 1024 * lax.rem(z + lax.div(a, 2), 4) + BLOCK * par + 256 * lax.rem(a, 2)
                valids.append(first_t + m >= 0)
        cache = [{} for _ in range(GROUP)]

        def term(u, c):
            v = (nj_ref[:, c * 128 : (c + 1) * 128] + nts[u]) - here[c, u * 8 : u * 8 + 8, :]
            return jnp.where(valids[u], v, 0.0) if halo else v

        def rolled(u, c):
            if c == 32:
                return jnp.zeros((8, 128), F32)
            low = c - c % 2
            if low not in cache[u]:
                both = jnp.concatenate([term(u, low), term(u, low + 1)], 0).astype(BF16)
                both = pltpu.roll(both, shifts[u], 1).astype(F32)
                cache[u][low], cache[u][low + 1] = both[:8], both[8:]
            return cache[u][c]

        for cd in range(33):
            col = slice(cd * 128, (cd + 1) * 128)
            s = carry_ref[:, col]
            for u in range(GROUP):
                row = slice(u * 8, u * 8 + 8)
                d = jnp.where(masks[u], rolled(u, (cd + base) % 33), rolled(u, (cd + base + 1) % 33))
                if halo:
                    s = s + d
                else:
                    s = s + (d - ring[row, col])
                    sums[row, col] = s
                ring[row, col] = d
            carry_ref[:, col] = s

    def look_up(i, u):
        mi = i * GROUP + u
        p = nb_ref[mi] - (m0 + mi)
        p = jnp.where(p < 0, p + PAD, p)
        hi = lax.shift_right_logical(p, 7)
        lo = p & 127
        sums = s_ref.at[i]
        accs = []
        for part in range(3):
            acc = jnp.zeros((8, 128), F32)
            for cd in range(part * 11, part * 11 + 11):
                g = jnp.take_along_axis(sums[u * 8 : u * 8 + 8, cd * 128 : (cd + 1) * 128], lo, axis=1, mode="promise_in_bounds")
                acc = jnp.where(hi == cd, g, acc)
            accs.append(acc)
        acc_ref[pl.ds(pl.multiple_of(mi * 8, 8), 8), :] = jnp.where(hi < 11, accs[0], jnp.where(hi < 22, accs[1], accs[2]))

    def windows(base, halo):
        def body(i, carry):
            window_sums(base, halo, i)
            return carry

        lax.fori_loop(0, MB // GROUP, body, 0)

    pl.when(step < 2)(functools.partial(windows, -1, True))
    pl.when((step >= 2) & (step < 6))(functools.partial(windows, 0, False))
    pl.when(step >= 6)(functools.partial(windows, 1, False))

    @pl.when(step >= 2)
    def _():
        def body(i, carry):
            for u in range(GROUP):
                look_up(i, u)
            return carry

        lax.fori_loop(0, MB // GROUP, body, 0)
        for a in range(8):
            for k in range(MB // 8):
                out_ref[a, k * 8 : (k + 1) * 8, :] = acc_ref[pl.ds(k * 64 + a, 8, stride=8), :]


def pick(where, own, other, nb):
    anywhere = pl.BlockSpec(memory_space=pl.ANY)
    return pl.pallas_call(
        pick_kernel,
        grid_spec=pltpu.PrefetchScalarGridSpec(
            num_scalar_prefetch=1,
            grid=(10,),
            in_specs=[anywhere] * 8
            + [
                pl.BlockSpec((MB, 8, 128), lambda i, w: (jnp.maximum(i - 2, 0), 0, 0)),
            ],
            out_specs=pl.BlockSpec((8, MB, 128), lambda i, w: (0, jnp.maximum(i - 2, 0), 0)),
            scratch_shapes=[
                pltpu.VMEM((SNAPS, BLOCK), BF16),
                pltpu.VMEM((8, SNAPS), F32),
                pltpu.VMEM((256, 128), F32),
                pltpu.VMEM((32, 256, 128), F32),
                pltpu.VMEM((256, 256), BF16),
                pltpu.VMEM((LAGS // GROUP, 8 * GROUP, PAD), F32),
                pltpu.VMEM((MB // GROUP, 8 * GROUP, PAD), F32),
                pltpu.VMEM((8, PAD), F32),
                pltpu.VMEM((256, 128), F32),
                pltpu.SemaphoreType.DMA((8,)),
            ],
        ),
        out_shape=jax.ShapeDtypeStruct((8, 256, 128), F32),
        compiler_params=pltpu.CompilerParams(vmem_limit_bytes=40 * 1024 * 1024),
        name="pick",
    )(where, *own, *other, nb)


def slot_map_kernel(nb_ref, out_ref):
    sub32 = lax.broadcasted_iota(jnp.int32, (32, 128), 0)
    sub128 = lax.broadcasted_iota(jnp.int32, (128, 128), 0)
    number = lax.broadcasted_iota(jnp.int32, (32, 128), 1).astype(F32) + 1.0

    def body(t, carry):
        nb = nb_ref[pl.ds(t, 1), :]
        hi = jnp.broadcast_to(lax.shift_right_logical(nb, 7), (32, 128))
        lo = jnp.broadcast_to(nb & 127, (128, 128))
        left = jnp.where(sub32 == hi, number, 0.0).astype(BF16)
        right = jnp.where(sub128 == lo, 1.0, 0.0).astype(BF16)
        r = lax.dot_general(left, right, NT, preferred_element_type=F32).astype(jnp.int32)
        for k in range(4):
            out_ref[pl.ds(lax.div(t, 8) * 256 + k * 64 + lax.rem(t, 8), 8, stride=8), :] = r[k * 8 : k * 8 + 8, :]
        return carry

    lax.fori_loop(0, 64, body, 0, unroll=8)


def slot_map(nb):
    return pl.pallas_call(
        slot_map_kernel,
        grid=(8,),
        in_specs=[pl.BlockSpec((64, 128), lambda i: (i, 0))],
        out_specs=pl.BlockSpec((2048, 128), lambda i: (i, 0)),
        out_shape=jax.ShapeDtypeStruct((BLOCK * 32, 128), jnp.int32),
        cost_estimate=pl.CostEstimate(flops=1 << 20, bytes_accessed=1 << 20, transcendentals=0),
        name="slot_map",
    )(nb)


def split3(x):
    hi = x.astype(BF16)
    rest = x - hi.astype(F32)
    mid = rest.astype(BF16)
    return hi, mid, (rest - mid.astype(F32)).astype(BF16)


def times_transposed(parts, hi, lo):
    r = lax.dot_general(parts, hi, NT, preferred_element_type=F32)
    q = lax.dot_general(parts[:64], lo, NT, preferred_element_type=F32)
    return ((r[64:] + q[32:]) + (r[32:64] + q[:32])) + r[:32]


def store_image(image, out_ref, steps):
    width = BLOCK // steps
    i = pl.program_id(0)
    out_ref[:, pl.ds(pl.multiple_of(i * width, width), width)] = image

    @pl.when(i == steps - 1)
    def _():
        v = out_ref[:, :BLOCK]
        rows = jnp.concatenate([v, jnp.zeros((96, BLOCK), F32)], 0)
        out_ref[:, BLOCK:] = lax.dot_general(
            v, rows, NT, precision=lax.Precision.HIGHEST, preferred_element_type=F32
        )


def operator_kernel(sum_ref, map_ref, b_ref, hi_ref, lo_ref, out_ref):
    kernel = 1.0 / (1.0 + sum_ref[...] * (2.0 / (LAGS * FEATURES)))
    mass = jnp.sum(kernel, axis=1, keepdims=True)
    markov = kernel / mass
    for g in range(8):
        w = [markov[g * 16 + h * 8 : g * 16 + h * 8 + 8, :] for h in range(2)]
        for c in range(32):
            col = slice(c * 128, (c + 1) * 128)
            values = []
            for h in range(2):
                first = (g * 2 + h) * 256 + c * 8
                at = map_ref[first : first + 8, :]
                value = jnp.take_along_axis(w[h], (at - 1) & 127, axis=1, mode="promise_in_bounds")
                values.append(jnp.where(at > 0, value, 0.0))
            v = jnp.concatenate(values, 0)
            hi = v.astype(BF16)
            hi_ref[g * 16 : (g + 1) * 16, col] = hi
            lo_ref[g * 16 : (g + 1) * 16, col] = (v - hi.astype(F32)).astype(BF16)
    image = times_transposed(jnp.concatenate(split3(b_ref[...]), 0), hi_ref[...], lo_ref[...])
    store_image(image, out_ref, 4)


def operator(total, slots, start):
    return pl.pallas_call(
        operator_kernel,
        grid=(4,),
        in_specs=[
            pl.BlockSpec((128, 128), lambda i: (i, 0)),
            pl.BlockSpec((4096, 128), lambda i: (i, 0)),
            pl.BlockSpec((32, SNAPS), lambda i: (0, 0)),
        ],
        out_specs=[
            pl.BlockSpec((128, SNAPS), lambda i: (i, 0)),
            pl.BlockSpec((128, SNAPS), lambda i: (i, 0)),
            pl.BlockSpec((32, BLOCK + 128), lambda i: (0, 0)),
        ],
        out_shape=[
            jax.ShapeDtypeStruct((BLOCK, SNAPS), BF16),
            jax.ShapeDtypeStruct((BLOCK, SNAPS), BF16),
            jax.ShapeDtypeStruct((32, BLOCK + 128), F32),
        ],
        name="operator",
    )(total, slots, start)


def apply_kernel(hi_ref, lo_ref, *refs):
    pieces, out_ref = refs[:-1], refs[-1]
    halves = len(pieces)
    full = jnp.concatenate([p[:, : SNAPS // halves] for p in pieces], 1)
    store_image(times_transposed(jnp.concatenate(split3(full), 0), hi_ref[...], lo_ref[...]), out_ref, 2)


def apply_rows(hi, lo, pieces):
    whole = pl.BlockSpec((32, pieces[0].shape[1]), lambda i: (0, 0))
    return pl.pallas_call(
        apply_kernel,
        grid=(2,),
        in_specs=[pl.BlockSpec((256, SNAPS), lambda i: (i, 0))] * 2 + [whole] * len(pieces),
        out_specs=pl.BlockSpec((32, BLOCK + 128), lambda i: (0, 0)),
        out_shape=jax.ShapeDtypeStruct((32, BLOCK + 128), F32),
        name="apply",
    )(hi, lo, *pieces)


def sum_four(v, axis, perms):
    r1, r2, r3 = [lax.ppermute(v, axis, p) for p in perms]
    v, r1, r2, r3 = [a.astype(F32) for a in (v, r1, r2, r3)]
    return (v + r2) + (r1 + r3)


def mul(a, b, dims=(((1,), (0,)), ((), ()))):
    return lax.dot_general(a, b, dims, precision=lax.Precision.HIGHEST, preferred_element_type=F32)


def shards(snapshots, neighbours, start_basis):
    row_at = lax.axis_index("row")
    z = row_at // 2
    par = row_at % 2
    z_send = [row_perm(d, 0) for d in (1, 2, 3)]
    core_swap = row_perm(0, 1)
    width = snapshots.shape[1] // 4

    def piece(d):
        at = ((z + d) % 4) * width
        return lax.dynamic_slice_in_dim(snapshots, at, width, 1)

    nb16 = neighbours.astype(jnp.int16)
    nb_from = [neighbours] + [None] * 3
    for d in (1, 2, 3):
        nb_from[4 - d] = lax.ppermute(nb16, "row", z_send[d - 1])
    own = [piece(0)] + [None] * 3
    for d in (2, 1, 3):
        own[4 - d] = lax.ppermute(piece(d), "row", z_send[d - 1])
    other = [lax.ppermute(a, "row", core_swap) for a in own]
    block = neighbours // BLOCK
    relative = (((block % 2) ^ par) * 4 + ((block // 2 - z) % 4)) * BLOCK + neighbours % BLOCK
    slots = slot_map(relative)
    order = jnp.arange(8, dtype=jnp.int32)
    order = 2 * ((order % 4 + z) % 4) + ((order // 4) ^ par)
    start = jnp.take(start_basis.reshape(32, 8, BLOCK), order, axis=1).reshape(32, SNAPS)

    where = jnp.stack([z, par]).astype(jnp.int32)
    nb_all = jnp.stack([a.astype(jnp.int32) for a in nb_from]).reshape(8, 256, 128).transpose(1, 0, 2)
    where, slots = lax.optimization_barrier((where, slots))
    chosen = pick(where, own, other, nb_all).reshape(4, BLOCK, 128)

    sent = chosen.astype(BF16)
    r1, r2, r3 = [lax.ppermute(sent[d], "row", z_send[d - 1]) for d in (1, 2, 3)]
    total = (chosen[0] + r2.astype(F32)) + (r1.astype(F32) + r3.astype(F32))
    total = sum_four(total.astype(BF16), "col", [col_perm(0, d) for d in (1, 2, 3)])
    total = sum_four(total, "col", [col_perm(d, 0) for d in (1, 2, 3)])

    def gather_all(v):
        parts = [v] + [None] * 3
        for d in (1, 2, 3):
            parts[4 - d] = lax.ppermute(v, "row", z_send[d - 1])
        gram = (parts[0][:, BLOCK:] + parts[2][:, BLOCK:]) + (parts[1][:, BLOCK:] + parts[3][:, BLOCK:])
        near = jnp.concatenate([p[:, :BLOCK] for p in parts] + [gram], 1)
        far = lax.ppermute(near, "row", core_swap)
        return (near, far), (gram + far[:, SNAPS // 2 :])[:, :32]

    hi, lo, image1 = operator(total, slots, start)
    full1, gram1 = gather_all(image1)
    image2 = apply_rows(hi, lo, full1)
    full2, gram2 = gather_all(image2)
    image3 = apply_rows(hi, lo, full2)[:, :BLOCK]
    image2 = image2[:, :BLOCK]
    cross = mul(image2, image3, NT)
    cross = sum_four(cross, "row", z_send)
    cross = cross + lax.ppermute(cross, "row", core_swap)

    eye = jnp.eye(32, dtype=F32)
    lower1 = jnp.linalg.cholesky(gram1 / SNAPS)
    inv1 = jax.scipy.linalg.solve_triangular(lower1, eye, lower=True)
    lower2 = jnp.linalg.cholesky(mul(mul(inv1, gram2), inv1, NT) / SNAPS)
    inv = mul(jax.scipy.linalg.solve_triangular(lower2, eye, lower=True), inv1)
    basis = mul(inv, image2)
    rayleigh = mul(mul(inv, cross), inv, NT) / SNAPS
    return basis, rayleigh


def solution(mesh):
    placed = (P("row", "col"), P("row", None), P())
    return jax.shard_map(
        shards, mesh=mesh, in_specs=placed, out_specs=(P(None, "row"), P()), check_vma=False
    )
```

```python
import functools

import jax
import jax.numpy as jnp
from jax import lax
from jax.experimental import pallas as pl
from jax.experimental.pallas import tpu as pltpu
from jax.sharding import PartitionSpec as P

SNAPS = 4096
FEATURES = 32768
LAGS = 64
BLOCK = 512
MB = 32
PAD = SNAPS + 128
GROUP = 16
NT = (((1,), (1,)), ((), ()))
F32 = jnp.float32
BF16 = jnp.bfloat16


def row_perm(step, flip):
    return [(2 * z + c, 2 * ((z + step) % 4) + (c ^ flip)) for z in range(4) for c in range(2)]


def col_perm(dy, dx):
    return [(4 * y + x, 4 * ((y + dy) % 4) + (x + dx) % 4) for y in range(4) for x in range(4)]


def squares(x):
    f = x.astype(F32)
    q = f * f
    hi = q.astype(BF16)
    return hi, (q - hi.astype(F32)).astype(BF16)


def pick_kernel(where_ref, p0, p1, p2, p3, q0, q1, q2, q3, nb_ref, out_ref, x_ref, nj_ref, nt_ref, g_ref, perm_ref, ring_ref, s_ref, carry_ref, acc_ref, sem):
    step = pl.program_id(0)
    z = where_ref[0]
    par = where_ref[1]
    lane = lax.broadcasted_iota(jnp.int32, (8, 128), 1)
    m0 = (step - 2) * MB

    def block_rows(d, parity):
        b = 2 * lax.rem(z + d, 4) + parity
        return pl.ds(pl.multiple_of(b * BLOCK, BLOCK), BLOCK)

    @pl.when(step == 0)
    def _():
        copies = []
        for d, (p, q) in enumerate(((p0, q0), (p1, q1), (p2, q2), (p3, q3))):
            copies.append(pltpu.make_async_copy(p, x_ref.at[block_rows(d, par)], sem.at[d]))
            copies.append(pltpu.make_async_copy(q, x_ref.at[block_rows(d, 1 - par)], sem.at[4 + d]))
        for c in copies:
            c.start()
        carry_ref[...] = jnp.zeros_like(carry_ref)
        ri = lax.broadcasted_iota(jnp.int32, (256, 256), 0)
        ci = lax.broadcasted_iota(jnp.int32, (256, 256), 1)
        perm_ref[...] = jnp.where(ci == lax.rem(ri, 8) * MB + lax.div(ri, 8), 1.0, 0.0).astype(BF16)
        for c in copies:
            c.wait()
        halves = jnp.full((8, BLOCK), 0.5, BF16)
        for b in range(16):
            hi, lo = squares(x_ref[b * 256 : (b + 1) * 256, :])
            nj_ref[:, b * 256 : (b + 1) * 256] = lax.dot_general(
                halves, hi, NT, preferred_element_type=F32
            ) + lax.dot_general(halves, lo, NT, preferred_element_type=F32)

    rows = []
    for a in range(8):
        t = 1024 * lax.rem(z + a // 2, 4) + BLOCK * par + 256 * (a % 2) + m0
        rows.append(x_ref[pl.ds(pl.multiple_of(jnp.maximum(t, 0), MB), MB), :])
    lhs = jnp.dot(perm_ref[...], jnp.concatenate(rows, 0), preferred_element_type=F32).astype(BF16)
    halves = jnp.full((BLOCK, 128), 0.5, BF16)
    hi, lo = squares(lhs)
    nt_ref[...] = jnp.dot(hi, halves, preferred_element_type=F32) + jnp.dot(lo, halves, preferred_element_type=F32)
    for jb in range(8):
        r = lax.dot_general(lhs, x_ref[jb * BLOCK : (jb + 1) * BLOCK, :], NT, preferred_element_type=F32)
        for k in range(4):
            g_ref[jb * 4 + k] = r[:, k * 128 : (k + 1) * 128]

    def window_sums(base, halo, i):
        shifts, masks, nts, valids = [], [], [], []
        ring = ring_ref.at[lax.rem(step, LAGS // MB) * (MB // GROUP) + i]
        sums = s_ref.at[i]
        here = g_ref.at[:, pl.ds(pl.multiple_of(i * (8 * GROUP), 8 * GROUP), 8 * GROUP), :]
        nt_here = nt_ref.at[pl.ds(pl.multiple_of(i * (8 * GROUP), 8 * GROUP), 8 * GROUP), :]
        for u in range(GROUP):
            m = m0 + i * GROUP + u
            shifts.append(lax.rem(256 - lax.rem(m + 128, 128), 128))
            masks.append(lane < 128 - lax.rem(m + 128, 128))
            nts.append(nt_here[u * 8 : u * 8 + 8, :])
            if halo:
                a = lax.broadcasted_iota(jnp.int32, (8, 128), 0)
                first_t = 1024 * lax.rem(z + lax.div(a, 2), 4) + BLOCK * par + 256 * lax.rem(a, 2)
                valids.append(first_t + m >= 0)
        cache = [{} for _ in range(GROUP)]

        def term(u, c):
            v = (nj_ref[:, c * 128 : (c + 1) * 128] + nts[u]) - here[c, u * 8 : u * 8 + 8, :]
            return jnp.where(valids[u], v, 0.0) if halo else v

        def rolled(u, c):
            if c == 32:
                return jnp.zeros((8, 128), F32)
            low = c - c % 2
            if low not in cache[u]:
                both = jnp.concatenate([term(u, low), term(u, low + 1)], 0).astype(BF16)
                both = pltpu.roll(both, shifts[u], 1).astype(F32)
                cache[u][low], cache[u][low + 1] = both[:8], both[8:]
            return cache[u][c]

        for cd in range(33):
            col = slice(cd * 128, (cd + 1) * 128)
            s = carry_ref[:, col]
            for u in range(GROUP):
                row = slice(u * 8, u * 8 + 8)
                d = jnp.where(masks[u], rolled(u, (cd + base) % 33), rolled(u, (cd + base + 1) % 33))
                if halo:
                    s = s + d
                else:
                    s = s + (d - ring[row, col])
                    sums[row, col] = s
                ring[row, col] = d
            carry_ref[:, col] = s

    def look_up(i, u):
        mi = i * GROUP + u
        p = nb_ref[mi] - (m0 + mi)
        p = jnp.where(p < 0, p + PAD, p)
        hi = lax.shift_right_logical(p, 7)
        lo = p & 127
        sums = s_ref.at[i]
        accs = []
        for part in range(3):
            acc = jnp.zeros((8, 128), F32)
            for cd in range(part * 11, part * 11 + 11):
                g = jnp.take_along_axis(sums[u * 8 : u * 8 + 8, cd * 128 : (cd + 1) * 128], lo, axis=1, mode="promise_in_bounds")
                acc = jnp.where(hi == cd, g, acc)
            accs.append(acc)
        acc_ref[pl.ds(pl.multiple_of(mi * 8, 8), 8), :] = jnp.where(hi < 11, accs[0], jnp.where(hi < 22, accs[1], accs[2]))

    def windows(base, halo):
        def body(i, carry):
            window_sums(base, halo, i)
            return carry

        lax.fori_loop(0, MB // GROUP, body, 0)

    pl.when(step < 2)(functools.partial(windows, -1, True))
    pl.when((step >= 2) & (step < 6))(functools.partial(windows, 0, False))
    pl.when(step >= 6)(functools.partial(windows, 1, False))

    @pl.when(step >= 2)
    def _():
        def body(i, carry):
            for u in range(GROUP):
                look_up(i, u)
            return carry

        lax.fori_loop(0, MB // GROUP, body, 0)
        for a in range(8):
            for k in range(MB // 8):
                out_ref[a, k * 8 : (k + 1) * 8, :] = acc_ref[pl.ds(k * 64 + a, 8, stride=8), :]


def pick(where, own, other, nb):
    anywhere = pl.BlockSpec(memory_space=pl.ANY)
    return pl.pallas_call(
        pick_kernel,
        grid_spec=pltpu.PrefetchScalarGridSpec(
            num_scalar_prefetch=1,
            grid=(10,),
            in_specs=[anywhere] * 8
            + [
                pl.BlockSpec((MB, 8, 128), lambda i, w: (jnp.maximum(i - 2, 0), 0, 0)),
            ],
            out_specs=pl.BlockSpec((8, MB, 128), lambda i, w: (0, jnp.maximum(i - 2, 0), 0)),
            scratch_shapes=[
                pltpu.VMEM((SNAPS, BLOCK), BF16),
                pltpu.VMEM((8, SNAPS), F32),
                pltpu.VMEM((256, 128), F32),
                pltpu.VMEM((32, 256, 128), F32),
                pltpu.VMEM((256, 256), BF16),
                pltpu.VMEM((LAGS // GROUP, 8 * GROUP, PAD), F32),
                pltpu.VMEM((MB // GROUP, 8 * GROUP, PAD), F32),
                pltpu.VMEM((8, PAD), F32),
                pltpu.VMEM((256, 128), F32),
                pltpu.SemaphoreType.DMA((8,)),
            ],
        ),
        out_shape=jax.ShapeDtypeStruct((8, 256, 128), F32),
        compiler_params=pltpu.CompilerParams(vmem_limit_bytes=40 * 1024 * 1024),
        name="pick",
    )(where, *own, *other, nb)


def slot_map_kernel(nb_ref, out_ref):
    sub32 = lax.broadcasted_iota(jnp.int32, (32, 128), 0)
    sub128 = lax.broadcasted_iota(jnp.int32, (128, 128), 0)
    number = lax.broadcasted_iota(jnp.int32, (32, 128), 1).astype(F32) + 1.0

    def body(t, carry):
        nb = nb_ref[pl.ds(t, 1), :]
        hi = jnp.broadcast_to(lax.shift_right_logical(nb, 7), (32, 128))
        lo = jnp.broadcast_to(nb & 127, (128, 128))
        left = jnp.where(sub32 == hi, number, 0.0).astype(BF16)
        right = jnp.where(sub128 == lo, 1.0, 0.0).astype(BF16)
        r = lax.dot_general(left, right, NT, preferred_element_type=F32).astype(jnp.int32)
        for k in range(4):
            out_ref[pl.ds(lax.div(t, 8) * 256 + k * 64 + lax.rem(t, 8), 8, stride=8), :] = r[k * 8 : k * 8 + 8, :]
        return carry

    lax.fori_loop(0, 64, body, 0, unroll=8)


def slot_map(nb):
    return pl.pallas_call(
        slot_map_kernel,
        grid=(8,),
        in_specs=[pl.BlockSpec((64, 128), lambda i: (i, 0))],
        out_specs=pl.BlockSpec((2048, 128), lambda i: (i, 0)),
        out_shape=jax.ShapeDtypeStruct((BLOCK * 32, 128), jnp.int32),
        cost_estimate=pl.CostEstimate(flops=1 << 20, bytes_accessed=1 << 20, transcendentals=0),
        name="slot_map",
    )(nb)


def split3(x):
    hi = x.astype(BF16)
    rest = x - hi.astype(F32)
    mid = rest.astype(BF16)
    return hi, mid, (rest - mid.astype(F32)).astype(BF16)


def times_transposed(parts, hi, lo):
    r = lax.dot_general(parts, hi, NT, preferred_element_type=F32)
    q = lax.dot_general(parts[:64], lo, NT, preferred_element_type=F32)
    return ((r[64:] + q[32:]) + (r[32:64] + q[:32])) + r[:32]


def store_image(image, out_ref, steps):
    width = BLOCK // steps
    i = pl.program_id(0)
    out_ref[:, pl.ds(pl.multiple_of(i * width, width), width)] = image

    @pl.when(i == steps - 1)
    def _():
        v = out_ref[:, :BLOCK]
        rows = jnp.concatenate([v, jnp.zeros((96, BLOCK), F32)], 0)
        out_ref[:, BLOCK:] = lax.dot_general(
            v, rows, NT, precision=lax.Precision.HIGHEST, preferred_element_type=F32
        )


def operator_kernel(sum_ref, map_ref, b_ref, hi_ref, lo_ref, out_ref):
    kernel = 1.0 / (1.0 + sum_ref[...] * (2.0 / (LAGS * FEATURES)))
    mass = jnp.sum(kernel, axis=1, keepdims=True)
    markov = kernel / mass
    for g in range(8):
        w = [markov[g * 16 + h * 8 : g * 16 + h * 8 + 8, :] for h in range(2)]
        for c in range(32):
            col = slice(c * 128, (c + 1) * 128)
            values = []
            for h in range(2):
                first = (g * 2 + h) * 256 + c * 8
                at = map_ref[first : first + 8, :]
                value = jnp.take_along_axis(w[h], (at - 1) & 127, axis=1, mode="promise_in_bounds")
                values.append(jnp.where(at > 0, value, 0.0))
            v = jnp.concatenate(values, 0)
            hi = v.astype(BF16)
            hi_ref[g * 16 : (g + 1) * 16, col] = hi
            lo_ref[g * 16 : (g + 1) * 16, col] = (v - hi.astype(F32)).astype(BF16)
    image = times_transposed(jnp.concatenate(split3(b_ref[...]), 0), hi_ref[...], lo_ref[...])
    store_image(image, out_ref, 4)


def operator(total, slots, start):
    return pl.pallas_call(
        operator_kernel,
        grid=(4,),
        in_specs=[
            pl.BlockSpec((128, 128), lambda i: (i, 0)),
            pl.BlockSpec((4096, 128), lambda i: (i, 0)),
            pl.BlockSpec((32, SNAPS), lambda i: (0, 0)),
        ],
        out_specs=[
            pl.BlockSpec((128, SNAPS), lambda i: (i, 0)),
            pl.BlockSpec((128, SNAPS), lambda i: (i, 0)),
            pl.BlockSpec((32, BLOCK + 128), lambda i: (0, 0)),
        ],
        out_shape=[
            jax.ShapeDtypeStruct((BLOCK, SNAPS), BF16),
            jax.ShapeDtypeStruct((BLOCK, SNAPS), BF16),
            jax.ShapeDtypeStruct((32, BLOCK + 128), F32),
        ],
        name="operator",
    )(total, slots, start)


def apply_kernel(hi_ref, lo_ref, *refs):
    pieces, out_ref = refs[:-1], refs[-1]
    halves = len(pieces)
    full = jnp.concatenate([p[:, : SNAPS // halves] for p in pieces], 1)
    store_image(times_transposed(jnp.concatenate(split3(full), 0), hi_ref[...], lo_ref[...]), out_ref, 2)


def apply_rows(hi, lo, pieces):
    whole = pl.BlockSpec((32, pieces[0].shape[1]), lambda i: (0, 0))
    return pl.pallas_call(
        apply_kernel,
        grid=(2,),
        in_specs=[pl.BlockSpec((256, SNAPS), lambda i: (i, 0))] * 2 + [whole] * len(pieces),
        out_specs=pl.BlockSpec((32, BLOCK + 128), lambda i: (0, 0)),
        out_shape=jax.ShapeDtypeStruct((32, BLOCK + 128), F32),
        name="apply",
    )(hi, lo, *pieces)


def sum_four(v, axis, perms):
    r1, r2, r3 = [lax.ppermute(v, axis, p) for p in perms]
    v, r1, r2, r3 = [a.astype(F32) for a in (v, r1, r2, r3)]
    return (v + r2) + (r1 + r3)


def mul(a, b, dims=(((1,), (0,)), ((), ()))):
    return lax.dot_general(a, b, dims, precision=lax.Precision.HIGHEST, preferred_element_type=F32)


def shards(snapshots, neighbours, start_basis):
    row_at = lax.axis_index("row")
    z = row_at // 2
    par = row_at % 2
    z_send = [row_perm(d, 0) for d in (1, 2, 3)]
    core_swap = row_perm(0, 1)
    width = snapshots.shape[1] // 4

    def piece(d):
        at = ((z + d) % 4) * width
        return lax.dynamic_slice_in_dim(snapshots, at, width, 1)

    nb16 = neighbours.astype(jnp.int16)
    nb_from = [neighbours] + [None] * 3
    for d in (1, 2, 3):
        nb_from[4 - d] = lax.ppermute(nb16, "row", z_send[d - 1])
    own = [piece(0)] + [None] * 3
    for d in (2, 1, 3):
        own[4 - d] = lax.ppermute(piece(d), "row", z_send[d - 1])
    other = [lax.ppermute(a, "row", core_swap) for a in own]
    block = neighbours // BLOCK
    relative = (((block % 2) ^ par) * 4 + ((block // 2 - z) % 4)) * BLOCK + neighbours % BLOCK
    slots = slot_map(relative)
    order = jnp.arange(8, dtype=jnp.int32)
    order = 2 * ((order % 4 + z) % 4) + ((order // 4) ^ par)
    start = jnp.take(start_basis.reshape(32, 8, BLOCK), order, axis=1).reshape(32, SNAPS)

    where = jnp.stack([z, par]).astype(jnp.int32)
    nb_all = jnp.stack([a.astype(jnp.int32) for a in nb_from]).reshape(8, 256, 128).transpose(1, 0, 2)
    where, slots = lax.optimization_barrier((where, slots))
    chosen = pick(where, own, other, nb_all).reshape(4, BLOCK, 128)

    sent = chosen.astype(BF16)
    r1, r2, r3 = [lax.ppermute(sent[d], "row", z_send[d - 1]) for d in (1, 2, 3)]
    total = (chosen[0] + r2.astype(F32)) + (r1.astype(F32) + r3.astype(F32))
    total = sum_four(total.astype(BF16), "col", [col_perm(0, d) for d in (1, 2, 3)])
    total = sum_four(total.astype(BF16), "col", [col_perm(d, 0) for d in (1, 2, 3)])

    def gather_all(v):
        parts = [v] + [None] * 3
        for d in (1, 2, 3):
            parts[4 - d] = lax.ppermute(v, "row", z_send[d - 1])
        gram = (parts[0][:, BLOCK:] + parts[2][:, BLOCK:]) + (parts[1][:, BLOCK:] + parts[3][:, BLOCK:])
        near = jnp.concatenate([p[:, :BLOCK] for p in parts] + [gram], 1)
        far = lax.ppermute(near, "row", core_swap)
        return (near, far), (gram + far[:, SNAPS // 2 :])[:, :32]

    hi, lo, image1 = operator(total, slots, start)
    full1, gram1 = gather_all(image1)
    image2 = apply_rows(hi, lo, full1)
    full2, gram2 = gather_all(image2)
    image3 = apply_rows(hi, lo, full2)[:, :BLOCK]
    image2 = image2[:, :BLOCK]
    cross = mul(image2, image3, NT)
    cross = sum_four(cross, "row", z_send)
    cross = cross + lax.ppermute(cross, "row", core_swap)

    eye = jnp.eye(32, dtype=F32)
    lower1 = jnp.linalg.cholesky(gram1 / SNAPS)
    inv1 = jax.scipy.linalg.solve_triangular(lower1, eye, lower=True)
    lower2 = jnp.linalg.cholesky(mul(mul(inv1, gram2), inv1, NT) / SNAPS)
    inv = mul(jax.scipy.linalg.solve_triangular(lower2, eye, lower=True), inv1)
    basis = mul(inv, image2)
    rayleigh = mul(mul(inv, cross), inv, NT) / SNAPS
    return basis, rayleigh


def solution(mesh):
    placed = (P("row", "col"), P("row", None), P())
    return jax.shard_map(
        shards, mesh=mesh, in_specs=placed, out_specs=(P(None, "row"), P()), check_vma=False
    )
```
